32 devices in a mesh: rows: 8 (over y, x, core), feat: 4 (over z).
Axes of the slice: x: 2, y: 2, z: 4, core: 2. Of those that a mesh axis runs over, the one named last changes fastest.
Arguments:
- features: bfloat16 [1536, 16384], P('rows', 'feat'), may hold values from -0.5 to 0.5
- labels: int32 [1536], P('rows'), may hold values 0 or 1
- posterior: bfloat16 [16384], P('feat'), may hold values from -1 to 1
- prior_prec: float32 [16384], P('feat'), may hold values from 1 to 10
Outputs:
- hessian: float32 [16384, 16384], P('feat', 'rows')
- gradient: float32 [16384], P('feat')
The draws below stay inside these ranges and needn't reach their ends.
All inputs are finite; a program needn't handle non-finite values. No bound on the sum of `labels` on one device may be relied on, other than what follows from the above.
Results may differ from the reference program's by a relative error of at most 0.003.
Values may be sent and summed in bfloat16 or wider, within the bound.
A program may use at most 128 MiB of HBM per device.

```python
import math
import jax
import jax.numpy as jnp
from jax import lax

F = 16384
NROWS = 1536


def plant(result, key, least, largest):
    shape = result.shape
    spot = [jax.random.randint(jax.random.fold_in(key, axis), (), 0, shape[axis]) for axis in range(len(shape))]
    result = result.at[tuple(spot)].set(least)
    longest = shape.index(max(shape))
    spot[longest] = (spot[longest] + 1) % shape[longest]
    return result.at[tuple(spot)].set(largest)


def block_scale(rng, dims, cuts, least, largest):
    def one(position, blocks):
        steps = jax.random.uniform(jax.random.fold_in(jax.random.fold_in(rng, 6), position), (blocks,), jnp.float32, least / len(cuts), largest / len(cuts))
        return jnp.repeat(jnp.exp(steps), dims[position] // blocks).reshape((-1,) + (1,) * (len(dims) - position - 1))

    loudness = one(*cuts[0])
    for cut in cuts[1:]:
        loudness = loudness * one(*cut)
    return loudness


def bell_draw(key, shape, width, bound, pieces=(), kind=jnp.bfloat16):
    entries = jax.random.normal(key, shape, jnp.float32) * width
    if len(pieces) > 0:
        entries = block_scale(key, shape, pieces, -0.22, 0.18) * entries
    return jnp.clip(entries, min=-bound, max=bound).astype(kind)


def setup_inputs(seed: int = 0) -> dict:
    splits = jax.random.split(jax.random.key(seed), 5)
    features = bell_draw(splits[0], (NROWS, F), 0.0625, 0.5, ((0, 8), (1, 4)))
    labels = plant((jax.random.randint(splits[1], (NROWS,), 0, 3) < 1).astype(jnp.int32), jax.random.fold_in(splits[1], 1), 0, 1)
    posterior = bell_draw(splits[2], (F,), (F // 512 + 1) ** -0.5, 1.0, ((0, 4),))
    prior_prec = jnp.clip(jnp.exp(math.log(10.0) - 2.3025851 * jax.random.uniform(splits[3], (F,), jnp.float32) ** block_scale(splits[3], (F,), ((0, 4),), -0.2, 0.2)), 1.0, 10.0)
    return {"features": features, "labels": labels, "posterior": posterior, "prior_prec": prior_prec}


def reference(features, labels, posterior, prior_prec):
    margins = jnp.dot(features, posterior, preferred_element_type=jnp.float32)
    chance = jax.nn.sigmoid(margins)
    weight = (chance * (1.0 - chance)).astype(jnp.bfloat16)
    residual = (labels.astype(jnp.float32) - chance).astype(jnp.bfloat16)
    gradient = jnp.dot(residual, features, preferred_element_type=jnp.float32) - prior_prec * posterior.astype(jnp.float32)
    weighted = weight[:, None] * features
    hessian = lax.dot_general(weighted, features, (((0,), (0,)), ((), ())), preferred_element_type=jnp.float32)
    diagonal = jnp.arange(F, dtype=jnp.int32)
    hessian = hessian.at[diagonal, diagonal].add(prior_prec)
    return hessian, gradient
```

```python
import functools

import jax
import jax.numpy as jnp
from jax import lax
from jax.experimental import pallas as pl
from jax.experimental.pallas import tpu as pltpu
from jax.sharding import PartitionSpec as P

MESH = pl.DeviceIdType.MESH
SPLIT = 2


def gather_kernel(
    row_count, feat_count, x_ref, st_ref, all_ref, col_ref, stat_ref,
    ring, zs, zr, ps, pr, ds, dr, cs, cr, cl, ss, sr, ts, tr, lsem,
):
    r = lax.axis_index("rows")
    f = lax.axis_index("feat")
    n, width = x_ref.shape
    half = width // 2
    col_width = col_ref.shape[1]
    unit = min(col_width, half)
    per_half = half // unit
    per_owner = col_width // unit
    chips = row_count // 2
    bits = chips.bit_length() - 1
    part = n // SPLIT

    def rows_of(device):
        return pl.ds(pl.multiple_of(device * n, n), n)

    def remote(src, dst, send, recv, **where):
        return pltpu.make_async_remote_copy(
            src_ref=src, dst_ref=dst, send_sem=send, recv_sem=recv,
            device_id=where, device_id_type=MESH,
        )

    sends = []

    def go(copy):
        copy.start()
        sends.append(copy)

    def ring_slice(step, h, k):
        rows, cols = pl.ds(k * part, part), pl.ds(h * half, half)
        return x_ref.at[rows, cols] if step == 0 else ring.at[step - 1, rows, cols]

    def ring_copy(step, h, k):
        to = lax.rem(f + (1 if h == 0 else feat_count - 1), feat_count)
        return remote(
            ring_slice(step, h, k),
            ring.at[step, pl.ds(k * part, part), pl.ds(h * half, half)],
            zs.at[step, h, k], zr.at[step, h, k], feat=to,
        )

    def column_sends(step, h, k, start):
        block = lax.rem(f + (feat_count - step if h == 0 else step), feat_count)
        for u in range(per_half):
            inner = h * half + u * unit
            if width % col_width == 0:
                owner = block * (width // col_width) + inner // col_width
                offset = inner % col_width
                slot = offset // unit
            else:
                owner = (block * width + inner) // col_width
                slot = ((block * width + inner) % col_width) // unit
                offset = pl.multiple_of(slot * unit, unit)
            src = ring_slice(step, h, k).at[:, pl.ds(u * unit, unit)]
            dst = col_ref.at[
                pl.ds(pl.multiple_of(r * n + k * part, part), part), pl.ds(offset, unit)
            ]
            send = cs.at[step, h, k, u]

            @pl.when(owner != r)
            def _():
                copy = remote(src, dst, send, cr.at[r, slot, k], rows=owner)
                copy.start() if start else copy.wait_send()

            if start:
                @pl.when(owner == r)
                def _():
                    pltpu.make_async_copy(src, dst, cl.at[slot, k]).start()

    def order(h):
        return list(range(bits)) if h == 0 else list(range(bits))[::-1]

    def spread(h, stage, mask):
        bit = 1 << order(h)[stage]
        origin = r ^ (2 * mask)
        cols = pl.ds(h * half, half)
        src = x_ref.at[:, cols] if mask == 0 else all_ref.at[rows_of(origin), cols]
        return remote(
            src, all_ref.at[rows_of(origin), cols],
            ps.at[h, mask | bit], pr.at[h, mask | bit], rows=r ^ (2 * bit),
        )

    def partner(h, mask):
        origin = r ^ (2 * mask)
        cols = pl.ds(h * half, half)
        src = x_ref.at[:, cols] if mask == 0 else all_ref.at[rows_of(origin), cols]
        return remote(
            src, all_ref.at[rows_of(origin), cols],
            ds.at[h, mask], dr.at[h, mask], rows=r ^ 1,
        )

    def masks_before(h, stage):
        found = [0]
        for b in order(h)[:stage]:
            found += [m | (1 << b) for m in found]
        return found

    for k in range(SPLIT):
        for h in range(2):
            go(ring_copy(0, h, k))
    stat_local = pltpu.make_async_copy(st_ref, stat_ref.at[r, f], lsem.at[0])
    stat_local.start()
    for d in range(1, feat_count):
        go(remote(
            st_ref, stat_ref.at[r, f], ss.at[d], sr.at[d],
            feat=lax.rem(f + d, feat_count),
        ))
    for stage in range(bits):
        for h in range(2):
            go(spread(h, stage, 0))
    for h in range(2):
        go(partner(h, 0))
    own = pltpu.make_async_copy(x_ref, all_ref.at[rows_of(r)], lsem.at[1])
    own.start()
    for k in range(SPLIT):
        for h in range(2):
            column_sends(0, h, k, True)

    stat_local.wait()
    for d in range(1, feat_count):
        remote(
            st_ref, stat_ref.at[r, lax.rem(f + feat_count - d, feat_count)],
            ss.at[d], sr.at[d], feat=f,
        ).wait_recv()
    for d in range(1, row_count):
        go(remote(
            stat_ref.at[r], stat_ref.at[r], ts.at[d], tr.at[d],
            rows=lax.rem(r + d, row_count),
        ))

    def relay(stage):
        for h in range(2):
            bit = 1 << order(h)[stage]
            for m in masks_before(h, stage):
                mask = m | bit
                cols = pl.ds(h * half, half)
                remote(
                    x_ref.at[:, cols], all_ref.at[rows_of(r ^ (2 * mask)), cols],
                    ps.at[h, mask], pr.at[h, mask], rows=r,
                ).wait_recv()
                for later in range(stage + 1, bits):
                    go(spread(h, later, mask))
                go(partner(h, mask))

    for step in range(1, feat_count):
        for k in range(SPLIT):
            for h in range(2):
                ring_copy(step - 1, h, k).wait_recv()
                if step < feat_count - 1:
                    go(ring_copy(step, h, k))
                column_sends(step, h, k, True)
        if step <= bits:
            relay(step - 1)
    for stage in range(feat_count - 1, bits):
        relay(stage)

    for h in range(2):
        for mask in range(chips):
            cols = pl.ds(h * half, half)
            remote(
                x_ref.at[:, cols], all_ref.at[rows_of(r ^ (2 * mask) ^ 1), cols],
                ds.at[h, mask], dr.at[h, mask], rows=r,
            ).wait_recv()
    for d in range(1, row_count):
        origin = lax.rem(r + row_count - d, row_count)
        remote(
            stat_ref.at[origin], stat_ref.at[origin], ts.at[d], tr.at[d], rows=r
        ).wait_recv()
        for slot in range(per_owner):
            for k in range(SPLIT):
                dst = col_ref.at[
                    pl.ds(pl.multiple_of(origin * n + k * part, part), part),
                    pl.ds(slot * unit, unit),
                ]
                remote(
                    x_ref.at[pl.ds(0, part), pl.ds(0, unit)], dst,
                    cs.at[0, 0, 0, 0], cr.at[origin, slot, k], rows=r,
                ).wait_recv()
    for slot in range(per_owner):
        for k in range(SPLIT):
            dst = col_ref.at[
                pl.ds(pl.multiple_of(r * n + k * part, part), part),
                pl.ds(slot * unit, unit),
            ]
            pltpu.make_async_copy(
                x_ref.at[pl.ds(0, part), pl.ds(0, unit)], dst, cl.at[slot, k]
            ).wait()
    own.wait()
    for copy in sends:
        copy.wait_send()
    for step in range(feat_count):
        for k in range(SPLIT):
            for h in range(2):
                column_sends(step, h, k, False)


def gather(features, stats):
    row_count = lax.axis_size("rows")
    feat_count = lax.axis_size("feat")
    n, width = features.shape
    half = width // 2
    col_width = width * feat_count // row_count
    unit = min(col_width, half)
    chips = row_count // 2
    dma = pltpu.SemaphoreType.DMA
    return pl.pallas_call(
        functools.partial(gather_kernel, row_count, feat_count),
        out_shape=(
            jax.ShapeDtypeStruct((row_count * n, width), features.dtype),
            jax.ShapeDtypeStruct((row_count * n, col_width), features.dtype),
            jax.ShapeDtypeStruct((row_count, feat_count) + stats.shape, stats.dtype),
        ),
        in_specs=[pl.BlockSpec(memory_space=pltpu.VMEM)] * 2,
        out_specs=[pl.BlockSpec(memory_space=pl.ANY)] * 3,
        scratch_shapes=[
            pltpu.VMEM((feat_count - 1, n, width), features.dtype),
            dma((feat_count - 1, 2, SPLIT)), dma((feat_count - 1, 2, SPLIT)),
            dma((2, chips)), dma((2, chips)),
            dma((2, chips)), dma((2, chips)),
            dma((feat_count, 2, SPLIT, half // unit)),
            dma((row_count, col_width // unit, SPLIT)),
            dma((col_width // unit, SPLIT)),
            dma((feat_count,)), dma((feat_count,)),
            dma((row_count,)), dma((row_count,)),
            dma((2,)),
        ],
        compiler_params=pltpu.CompilerParams(
            has_side_effects=True, vmem_limit_bytes=32 * 1024 * 1024
        ),
        name="gather",
    )(features, stats)


def per_device(features, labels, posterior, prior_prec):
    row_count = lax.axis_size("rows")
    feat_count = lax.axis_size("feat")
    row_index = lax.axis_index("rows")
    feat_index = lax.axis_index("feat")
    n, block_width = features.shape
    col_width = block_width * feat_count // row_count
    partial_value = jnp.dot(features, posterior, preferred_element_type=jnp.float32)
    padded = -(-n // 512) * 512
    stats = jnp.concatenate([
        jnp.pad(partial_value, (0, padded - n)),
        jnp.pad(labels.astype(jnp.float32), (0, padded - n)),
    ]).reshape(-1, 128)
    all_rows, column_rows, all_stats = gather(features, stats)
    all_stats = all_stats.reshape(row_count, feat_count, 2, padded)[..., :n]
    margins = jnp.sum(all_stats[:, :, 0], axis=1).reshape(-1)
    all_labels = all_stats[:, 0, 1].reshape(-1)
    chance = jax.nn.sigmoid(margins)
    weight = (chance * (1.0 - chance)).astype(jnp.bfloat16)
    residual = (all_labels - chance).astype(jnp.bfloat16)
    summed = jnp.dot(residual, all_rows, preferred_element_type=jnp.float32)
    gradient = summed - prior_prec * posterior.astype(jnp.float32)
    weighted = weight[:, None] * all_rows
    product = lax.dot_general(
        weighted, column_rows, (((0,), (0,)), ((), ())), preferred_element_type=jnp.float32
    )
    global_rows = feat_index * block_width + jnp.arange(block_width, dtype=jnp.int32)
    global_cols = row_index * col_width + jnp.arange(col_width, dtype=jnp.int32)
    on_diagonal = global_rows[:, None] == global_cols[None, :]
    hessian = product + jnp.where(on_diagonal, prior_prec[:, None], jnp.float32(0.0))
    return (hessian, gradient)


def solution(mesh):
    in_specs = (P("rows", "feat"), P("rows"), P("feat"), P("feat"))
    out_specs = (P("feat", "rows"), P("feat"))
    return jax.shard_map(
        per_device, mesh=mesh, in_specs=in_specs, out_specs=out_specs, check_vma=False
    )
```

```python
import functools

import jax
import jax.numpy as jnp
from jax import lax
from jax.experimental import pallas as pl
from jax.experimental.pallas import tpu as pltpu
from jax.sharding import PartitionSpec as P

MESH = pl.DeviceIdType.MESH
SPLIT = 4


def gather_kernel(
    row_count, feat_count, x_ref, st_ref, all_ref, col_ref, stat_ref,
    ring, zs, zr, ps, pr, ds, dr, cs, cr, cl, ss, sr, ts, tr, lsem,
):
    r = lax.axis_index("rows")
    f = lax.axis_index("feat")
    n, width = x_ref.shape
    half = width // 2
    col_width = col_ref.shape[1]
    unit = min(col_width, half)
    per_half = half // unit
    per_owner = col_width // unit
    chips = row_count // 2
    bits = chips.bit_length() - 1
    part = n // SPLIT

    def rows_of(device):
        return pl.ds(pl.multiple_of(device * n, n), n)

    def remote(src, dst, send, recv, **where):
        return pltpu.make_async_remote_copy(
            src_ref=src, dst_ref=dst, send_sem=send, recv_sem=recv,
            device_id=where, device_id_type=MESH,
        )

    sends = []

    def go(copy):
        copy.start()
        sends.append(copy)

    def ring_slice(step, h, k):
        rows, cols = pl.ds(k * part, part), pl.ds(h * half, half)
        return x_ref.at[rows, cols] if step == 0 else ring.at[step - 1, rows, cols]

    def ring_copy(step, h, k):
        to = lax.rem(f + (1 if h == 0 else feat_count - 1), feat_count)
        return remote(
            ring_slice(step, h, k),
            ring.at[step, pl.ds(k * part, part), pl.ds(h * half, half)],
            zs.at[step, h, k], zr.at[step, h, k], feat=to,
        )

    def column_sends(step, h, k, start):
        block = lax.rem(f + (feat_count - step if h == 0 else step), feat_count)
        for u in range(per_half):
            inner = h * half + u * unit
            if width % col_width == 0:
                owner = block * (width // col_width) + inner // col_width
                offset = inner % col_width
                slot = offset // unit
            else:
                owner = (block * width + inner) // col_width
                slot = ((block * width + inner) % col_width) // unit
                offset = pl.multiple_of(slot * unit, unit)
            src = ring_slice(step, h, k).at[:, pl.ds(u * unit, unit)]
            dst = col_ref.at[
                pl.ds(pl.multiple_of(r * n + k * part, part), part), pl.ds(offset, unit)
            ]
            send = cs.at[step, h, k, u]

            @pl.when(owner != r)
            def _():
                copy = remote(src, dst, send, cr.at[r, slot, k], rows=owner)
                copy.start() if start else copy.wait_send()

            if start:
                @pl.when(owner == r)
                def _():
                    pltpu.make_async_copy(src, dst, cl.at[slot, k]).start()

    def order(h):
        return list(range(bits)) if h == 0 else list(range(bits))[::-1]

    def spread(h, stage, mask):
        bit = 1 << order(h)[stage]
        origin = r ^ (2 * mask)
        cols = pl.ds(h * half, half)
        src = x_ref.at[:, cols] if mask == 0 else all_ref.at[rows_of(origin), cols]
        return remote(
            src, all_ref.at[rows_of(origin), cols],
            ps.at[h, mask | bit], pr.at[h, mask | bit], rows=r ^ (2 * bit),
        )

    def partner(h, mask):
        origin = r ^ (2 * mask)
        cols = pl.ds(h * half, half)
        src = x_ref.at[:, cols] if mask == 0 else all_ref.at[rows_of(origin), cols]
        return remote(
            src, all_ref.at[rows_of(origin), cols],
            ds.at[h, mask], dr.at[h, mask], rows=r ^ 1,
        )

    def masks_before(h, stage):
        found = [0]
        for b in order(h)[:stage]:
            found += [m | (1 << b) for m in found]
        return found

    for k in range(SPLIT):
        for h in range(2):
            go(ring_copy(0, h, k))
    stat_local = pltpu.make_async_copy(st_ref, stat_ref.at[r, f], lsem.at[0])
    stat_local.start()
    for d in range(1, feat_count):
        go(remote(
            st_ref, stat_ref.at[r, f], ss.at[d], sr.at[d],
            feat=lax.rem(f + d, feat_count),
        ))
    for stage in range(bits):
        for h in range(2):
            go(spread(h, stage, 0))
    for h in range(2):
        go(partner(h, 0))
    own = pltpu.make_async_copy(x_ref, all_ref.at[rows_of(r)], lsem.at[1])
    own.start()
    for k in range(SPLIT):
        for h in range(2):
            column_sends(0, h, k, True)

    stat_local.wait()
    for d in range(1, feat_count):
        remote(
            st_ref, stat_ref.at[r, lax.rem(f + feat_count - d, feat_count)],
            ss.at[d], sr.at[d], feat=f,
        ).wait_recv()
    for d in range(1, row_count):
        go(remote(
            stat_ref.at[r], stat_ref.at[r], ts.at[d], tr.at[d],
            rows=lax.rem(r + d, row_count),
        ))

    def relay(stage):
        for h in range(2):
            bit = 1 << order(h)[stage]
            for m in masks_before(h, stage):
                mask = m | bit
                cols = pl.ds(h * half, half)
                remote(
                    x_ref.at[:, cols], all_ref.at[rows_of(r ^ (2 * mask)), cols],
                    ps.at[h, mask], pr.at[h, mask], rows=r,
                ).wait_recv()
                for later in range(stage + 1, bits):
                    go(spread(h, later, mask))
                go(partner(h, mask))

    for step in range(1, feat_count):
        for k in range(SPLIT):
            for h in range(2):
                ring_copy(step - 1, h, k).wait_recv()
                if step < feat_count - 1:
                    go(ring_copy(step, h, k))
                column_sends(step, h, k, True)
        if step <= bits:
            relay(step - 1)
    for stage in range(feat_count - 1, bits):
        relay(stage)

    for h in range(2):
        for mask in range(chips):
            cols = pl.ds(h * half, half)
            remote(
                x_ref.at[:, cols], all_ref.at[rows_of(r ^ (2 * mask) ^ 1), cols],
                ds.at[h, mask], dr.at[h, mask], rows=r,
            ).wait_recv()
    for d in range(1, row_count):
        origin = lax.rem(r + row_count - d, row_count)
        remote(
            stat_ref.at[origin], stat_ref.at[origin], ts.at[d], tr.at[d], rows=r
        ).wait_recv()
        for slot in range(per_owner):
            for k in range(SPLIT):
                dst = col_ref.at[
                    pl.ds(pl.multiple_of(origin * n + k * part, part), part),
                    pl.ds(slot * unit, unit),
                ]
                remote(
                    x_ref.at[pl.ds(0, part), pl.ds(0, unit)], dst,
                    cs.at[0, 0, 0, 0], cr.at[origin, slot, k], rows=r,
                ).wait_recv()
    for slot in range(per_owner):
        for k in range(SPLIT):
            dst = col_ref.at[
                pl.ds(pl.multiple_of(r * n + k * part, part), part),
                pl.ds(slot * unit, unit),
            ]
            pltpu.make_async_copy(
                x_ref.at[pl.ds(0, part), pl.ds(0, unit)], dst, cl.at[slot, k]
            ).wait()
    own.wait()
    for copy in sends:
        copy.wait_send()
    for step in range(feat_count):
        for k in range(SPLIT):
            for h in range(2):
                column_sends(step, h, k, False)


def gather(features, stats):
    row_count = lax.axis_size("rows")
    feat_count = lax.axis_size("feat")
    n, width = features.shape
    half = width // 2
    col_width = width * feat_count // row_count
    unit = min(col_width, half)
    chips = row_count // 2
    dma = pltpu.SemaphoreType.DMA
    return pl.pallas_call(
        functools.partial(gather_kernel, row_count, feat_count),
        out_shape=(
            jax.ShapeDtypeStruct((row_count * n, width), features.dtype),
            jax.ShapeDtypeStruct((row_count * n, col_width), features.dtype),
            jax.ShapeDtypeStruct((row_count, feat_count) + stats.shape, stats.dtype),
        ),
        in_specs=[pl.BlockSpec(memory_space=pltpu.VMEM)] * 2,
        out_specs=[pl.BlockSpec(memory_space=pl.ANY)] * 3,
        scratch_shapes=[
            pltpu.VMEM((feat_count - 1, n, width), features.dtype),
            dma((feat_count - 1, 2, SPLIT)), dma((feat_count - 1, 2, SPLIT)),
            dma((2, chips)), dma((2, chips)),
            dma((2, chips)), dma((2, chips)),
            dma((feat_count, 2, SPLIT, half // unit)),
            dma((row_count, col_width // unit, SPLIT)),
            dma((col_width // unit, SPLIT)),
            dma((feat_count,)), dma((feat_count,)),
            dma((row_count,)), dma((row_count,)),
            dma((2,)),
        ],
        compiler_params=pltpu.CompilerParams(
            has_side_effects=True, vmem_limit_bytes=32 * 1024 * 1024
        ),
        name="gather",
    )(features, stats)


def per_device(features, labels, posterior, prior_prec):
    row_count = lax.axis_size("rows")
    feat_count = lax.axis_size("feat")
    row_index = lax.axis_index("rows")
    feat_index = lax.axis_index("feat")
    n, block_width = features.shape
    col_width = block_width * feat_count // row_count
    partial_value = jnp.dot(features, posterior, preferred_element_type=jnp.float32)
    padded = -(-n // 512) * 512
    stats = jnp.concatenate([
        jnp.pad(partial_value, (0, padded - n)),
        jnp.pad(labels.astype(jnp.float32), (0, padded - n)),
    ]).reshape(-1, 128)
    all_rows, column_rows, all_stats = gather(features, stats)
    all_stats = all_stats.reshape(row_count, feat_count, 2, padded)[..., :n]
    margins = jnp.sum(all_stats[:, :, 0], axis=1).reshape(-1)
    all_labels = all_stats[:, 0, 1].reshape(-1)
    chance = jax.nn.sigmoid(margins)
    weight = (chance * (1.0 - chance)).astype(jnp.bfloat16)
    residual = (all_labels - chance).astype(jnp.bfloat16)
    summed = jnp.dot(residual, all_rows, preferred_element_type=jnp.float32)
    gradient = summed - prior_prec * posterior.astype(jnp.float32)
    weighted = weight[:, None] * all_rows
    product = lax.dot_general(
        weighted, column_rows, (((0,), (0,)), ((), ())), preferred_element_type=jnp.float32
    )
    global_rows = feat_index * block_width + jnp.arange(block_width, dtype=jnp.int32)
    global_cols = row_index * col_width + jnp.arange(col_width, dtype=jnp.int32)
    on_diagonal = global_rows[:, None] == global_cols[None, :]
    hessian = product + jnp.where(on_diagonal, prior_prec[:, None], jnp.float32(0.0))
    return (hessian, gradient)


def solution(mesh):
    in_specs = (P("rows", "feat"), P("rows"), P("feat"), P("feat"))
    out_specs = (P("feat", "rows"), P("feat"))
    return jax.shard_map(
        per_device, mesh=mesh, in_specs=in_specs, out_specs=out_specs, check_vma=False
    )
```
